128 devices in a mesh: inp: 32 (over y_hi, x, z), tm: 4 (over y_lo, core).
Axes of the slice: x: 4, y: 4 (y_hi: 2, y_lo: 2; y = y_hi * 2 + y_lo), z: 4, core: 2. Of those that a mesh axis runs over, the one named last changes fastest.
Arguments:
- voltages: float32 [256, 256, 2048], P('inp', 'tm'), may hold values from -6 to 6
- filter_taps: float32 [4, 2048], replicated, may hold values from -1 to 2
Outputs:
- visibilities: float32 [2, 1024, 256, 256], P(None, ('inp', 'tm'))
The draws below stay inside these ranges and needn't reach their ends.
All inputs are finite; a program needn't handle non-finite values.
Results may differ from the reference program's by a relative error of at most 0.000084.
Values sent between devices are 32-bit elements; how exact they have to be, the bound alone decides.
A program may use at most 128 MiB of HBM per device.

```python
import math
import jax
import jax.numpy as jnp
from jax import lax

NI = 256
NFFT = 2048
TAPS = 4
CH = 1024
SPECTRA = 256


def draw_filter_taps(key, part):
    total = TAPS * NFFT
    position = jnp.arange(total, dtype=jnp.float32).reshape(TAPS, NFFT)
    centre = (total - 1) / 2.0
    window = 0.5 - 0.5 * jnp.cos(2.0 * math.pi * (position + 0.5) / total)
    proto = jnp.sinc((position - centre) / NFFT) * window
    rough = jax.random.uniform(key, (TAPS, NFFT), jnp.float32, 0.5, 1.5)
    return (proto * rough).astype(jnp.float32)


def block_levels(rng, extent, split, smallest, high):
    level = 1.0
    for dim, blocks in split:
        heights = jax.random.uniform(jax.random.fold_in(jax.random.fold_in(rng, 6), dim), (blocks,), jnp.float32, smallest / len(split), high / len(split))
        level = level * jnp.repeat(jnp.exp(heights), extent[dim] // blocks).reshape((-1,) + (1,) * (len(extent) - 1 - dim))
    return level


def normal_values(stream_key, shape, scale, reach, pieces=(), kind=jnp.bfloat16):
    values = jax.random.normal(stream_key, shape, jnp.float32) * scale
    if len(pieces) > 0:
        values = block_levels(stream_key, shape, pieces, -0.22, 0.18) * values
    return jnp.clip(values, min=-reach, max=reach).astype(kind)


def setup_inputs(seed: int = 0) -> dict:
    seeds = jax.random.split(jax.random.key(seed), 3)
    voltages = normal_values(seeds[0], (NI, SPECTRA, NFFT), 1.0, 6.0, ((0, 32), (1, 4)), jnp.float32)
    filter_taps = draw_filter_taps(jax.random.fold_in(seeds[2], 71), 0)
    return dict(voltages=voltages, filter_taps=filter_taps)


def reference(voltages, filter_taps):
    zeros = jnp.zeros((NI, TAPS - 1, NFFT), voltages.dtype)
    frames = jnp.concatenate([zeros, voltages], axis=1)
    filtered = filter_taps[0] * frames[:, 0:SPECTRA, :]
    for k in range(1, TAPS):
        filtered = filtered + filter_taps[k] * frames[:, k:k + SPECTRA, :]
    spec = jnp.fft.rfft(filtered, axis=-1)[:, :, :CH]
    spec_re = jnp.transpose(jnp.real(spec), (2, 0, 1)) / math.sqrt(NFFT)
    spec_im = jnp.transpose(jnp.imag(spec), (2, 0, 1)) / math.sqrt(NFFT)
    spec_re = spec_re.astype(voltages.dtype)
    spec_im = spec_im.astype(voltages.dtype)
    left = jnp.concatenate([spec_re, spec_im], axis=-1)
    twisted = jnp.concatenate([spec_im, -spec_re], axis=-1)
    block = 16
    left_b = left.reshape(CH // block, block, NI, 2 * SPECTRA)
    twisted_b = twisted.reshape(CH // block, block, NI, 2 * SPECTRA)

    def correlate(pair):
        plain, turned = pair
        real_part = jnp.einsum('cas,cbs->cab', plain, plain, precision=lax.Precision.HIGHEST)
        imag_part = jnp.einsum('cas,cbs->cab', turned, plain, precision=lax.Precision.HIGHEST)
        return jnp.stack([real_part, imag_part])
    result = lax.map(correlate, (left_b, twisted_b))
    result = jnp.transpose(result, (1, 0, 2, 3, 4)).reshape(2, CH, NI, NI)
    return result / SPECTRA
```

```python
import functools
import math

import jax
import jax.numpy as jnp
import numpy as np
from jax import lax
from jax.experimental import pallas as pl
from jax.experimental.pallas import tpu as pltpu
from jax.sharding import PartitionSpec as P

LANES = 128
F32 = jnp.float32
BF16 = jnp.bfloat16


def tables(nfft, spectra):
    dests = 128
    n2 = np.arange(LANES)
    scale = 1.0 / math.sqrt(nfft) / math.sqrt(spectra)
    out = np.zeros((9, dests, 2 * LANES), np.float64)
    for r in range(9):
        for m in range(dests):
            if (r == 0 and m % 2 == 1) or (r == 8 and m % 2 == 0):
                continue
            q = m // 2 if (m % 2 == 0 or r == 8) else 127 - m // 2
            angle = 2.0 * np.pi * ((n2 * (16 * q + r)) % nfft) / nfft
            out[r, m, :LANES] = np.cos(angle) * scale
            out[r, m, LANES:] = np.sin(angle) * scale
    out = out.astype(np.float32)
    high = out.astype(jnp.bfloat16)
    low = (out - high.astype(np.float32)).astype(jnp.bfloat16)
    return np.concatenate([high, low], axis=1)


def split(value):
    high = value.astype(BF16)
    return high, (value - high.astype(F32)).astype(BF16)


def sixteen(x):
    c1, c2, c3 = (math.cos(k * math.pi / 8) for k in (1, 2, 3))
    a = [x[n] + x[n + 8] for n in range(8)]
    b = [x[n] - x[n + 8] for n in range(8)]
    c = [a[n] + a[n + 4] for n in range(4)]
    d = [a[n] - a[n + 4] for n in range(4)]
    c02, c13 = c[0] + c[2], c[1] + c[3]
    y = {0: (c02 + c13, None), 8: (c02 - c13, None), 4: (c[0] - c[2], c[3] - c[1])}
    dm, dp = (d[1] - d[3]) * c2, (d[1] + d[3]) * c2
    y[2] = (d[0] + dm, -(d[2] + dp))
    y[6] = (d[0] - dm, d[2] - dp)
    e = [None] + [b[n] - b[8 - n] for n in (1, 2, 3)]
    g = [None] + [b[n] + b[8 - n] for n in (1, 2, 3)]
    e2, g2 = e[2] * c2, g[2] * c2
    p, q = b[0] + e2, b[0] - e2
    s, t = e[1] * c1 + e[3] * c3, e[1] * c3 - e[3] * c1
    v, w = b[4] + g2, g2 - b[4]
    h, k = g[1] * c3 + g[3] * c1, g[1] * c1 - g[3] * c3
    y[1] = (p + s, -(v + h))
    y[7] = (p - s, v - h)
    y[3] = (q + t, -(k + w))
    y[5] = (q - t, w - k)
    return y


def contract(a, b):
    return lax.dot_general(a, b, (((1,), (1,)), ((), ())), preferred_element_type=F32)


def front_kernel(volt, halo, taps, table, send, ext, tapb, xs, sem):
    inputs, frames = volt.shape[0], volt.shape[1]
    blocks = volt.shape[2] // LANES
    copies = []
    for l in range(blocks):
        lanes = pl.ds(l * LANES, LANES)
        copies.append(pltpu.make_async_copy(volt.at[:, :, lanes], ext.at[:, l, pl.ds(8, frames), :], sem.at[l]))
        copies[-1].start()
    for k in range(4):
        for l in range(blocks):
            tapb[k, l] = jnp.broadcast_to(taps[k : k + 1, l * LANES : (l + 1) * LANES], (8, LANES))
    for i in range(inputs):
        for l in range(blocks):
            ext[i, l, 5:8, :] = halo[i, :, l * LANES : (l + 1) * LANES]
    for copy in copies:
        copy.wait()

    step = 16

    @pl.loop(0, inputs)
    def _(i):
        for f in range(frames // step):
            parts = []
            for l in range(blocks):
                halves = []
                for j in range(step // 8):
                    row = 5 + f * step + j * 8
                    acc = tapb[0, l] * ext[i, l, pl.ds(row, 8), :]
                    for k in range(1, 4):
                        acc = acc + tapb[k, l] * ext[i, l, pl.ds(row + k, 8), :]
                    halves.append(acc)
                parts.append(jnp.concatenate(halves, axis=0))
            y = sixteen(parts)
            rows = pl.ds(pl.multiple_of(i * frames, frames) + f * step, step)
            for r in range(9):
                real, imag = y[r]
                high, low = split(real)
                xs[r, 0, 0, rows, :] = high
                xs[r, 1, 0, rows, :] = low
                xs[r, 0, 1, rows, :] = -high
                xs[r, 1, 1, rows, :] = -low
                if imag is not None:
                    high, low = split(imag)
                    xs[r, 0, 2, rows, :] = high
                    xs[r, 1, 2, rows, :] = low

    def operand(r, part, pair):
        blocks_ = []
        for i in (2 * pair, 2 * pair + 1):
            rows = pl.ds(i * frames, frames)
            real, minus = xs[r, part, 0, rows, :], xs[r, part, 1, rows, :]
            imag = jnp.zeros_like(real) if r in (0, 8) else xs[r, part, 2, rows, :]
            blocks_.append(jnp.concatenate([real, imag], axis=1))
            blocks_.append(jnp.concatenate([imag, minus], axis=1))
        return jnp.concatenate(blocks_, axis=0)

    def product(r, pair):
        both = contract(table[r], operand(r, 0, pair))
        return both[:128] + both[128:] + contract(table[r, 0:128], operand(r, 1, pair))

    for r in range(8):
        for pair in range(inputs // 2):
            out = product(r, pair)
            if r == 0:
                out = out + product(8, pair)
            for h in range(2):
                send[pl.ds(r * inputs + 2 * pair + h, 128, stride=64), :] = out[:, h * LANES : (h + 1) * LANES]


def front(voltages, halo, taps, table):
    inputs, frames, nfft = voltages.shape
    vmem = pl.BlockSpec(memory_space=pltpu.VMEM)
    return pl.pallas_call(
        front_kernel,
        out_shape=jax.ShapeDtypeStruct((128 * 64, LANES), F32),
        in_specs=[pl.BlockSpec(memory_space=pl.ANY), vmem, vmem, vmem],
        out_specs=vmem,
        scratch_shapes=[
            pltpu.VMEM((inputs, nfft // LANES, frames + 8, LANES), F32),
            pltpu.VMEM((4, nfft // LANES, 8, LANES), F32),
            pltpu.VMEM((9, 2, 3, inputs * frames, LANES), BF16),
            pltpu.SemaphoreType.DMA((nfft // LANES,)),
        ],
        compiler_params=pltpu.CompilerParams(vmem_limit_bytes=48 << 20),
    )(voltages, halo, taps, table)


def correlate_kernel(recv, out):
    odd = lax.rem(lax.axis_index("tm"), 2)
    lane = lax.broadcasted_iota(jnp.int32, (256, LANES), 1)
    sign = jnp.where(lane < 64, 1.0, -1.0).astype(F32)
    for r in range(8):
        blocks, turns = [], []
        for t in range(4):
            block = recv[r, t]
            blocks.append(block)
            turns.append(pltpu.roll(block, 64, 1) * sign)
        plain = [split(b) for b in blocks]
        turned = [split(b) for b in turns]
        ph = jnp.concatenate([b[0] for b in plain], axis=1)
        plo = jnp.concatenate([b[1] for b in plain], axis=1)
        th = jnp.concatenate([b[0] for b in turned], axis=1)
        tlo = jnp.concatenate([b[1] for b in turned], axis=1)
        real = contract(ph, ph) + contract(ph, plo) + contract(plo, ph)
        imag = contract(th, ph) + contract(th, plo) + contract(tlo, ph)
        flip = 1.0 if r == 0 else jnp.where(odd == 1, -1.0, 1.0).astype(F32)
        chan = jnp.where(odd == 1, (8 - r) % 8, r)
        out[0, chan] = real
        out[1, chan] = imag * flip


def on_device(voltages, taps):
    frames = voltages.shape[1]
    table = jnp.asarray(tables(2048, 256))
    last = voltages[:, frames - 3 :, :]
    halo = lax.ppermute(last, "tm", [(0, 1), (1, 2), (2, 3)])
    send = front(voltages, halo, taps, table)
    got = lax.all_to_all(send.reshape(128, 8, 8, LANES), ("inp", "tm"), split_axis=0, concat_axis=0, tiled=True)
    got = got.reshape(32, 4, 8, 8, LANES).transpose(2, 1, 0, 3, 4).reshape(8, 4, 256, LANES)
    vmem = pl.BlockSpec(memory_space=pltpu.VMEM)
    return pl.pallas_call(
        correlate_kernel,
        out_shape=jax.ShapeDtypeStruct((2, 8, 256, 256), F32),
        in_specs=[vmem],
        out_specs=vmem,
        compiler_params=pltpu.CompilerParams(vmem_limit_bytes=48 << 20),
    )(got)


def solution(mesh):
    return jax.shard_map(
        on_device,
        mesh=mesh,
        in_specs=(P("inp", "tm", None), P()),
        out_specs=P(None, ("inp", "tm"), None, None),
        check_vma=False,
    )
```

```python
import functools
import math

import jax
import jax.numpy as jnp
import numpy as np
from jax import lax
from jax.experimental import pallas as pl
from jax.experimental.pallas import tpu as pltpu
from jax.sharding import PartitionSpec as P

LANES = 128
F32 = jnp.float32
BF16 = jnp.bfloat16


def tables(nfft, spectra):
    dests = 128
    n2 = np.arange(LANES)
    scale = 1.0 / math.sqrt(nfft) / math.sqrt(spectra)
    out = np.zeros((9, dests, 2 * LANES), np.float64)
    for r in range(9):
        for m in range(dests):
            if (r == 0 and m % 2 == 1) or (r == 8 and m % 2 == 0):
                continue
            q = m // 2 if (m % 2 == 0 or r == 8) else 127 - m // 2
            angle = 2.0 * np.pi * ((n2 * (16 * q + r)) % nfft) / nfft
            out[r, m, :LANES] = np.cos(angle) * scale
            out[r, m, LANES:] = np.sin(angle) * scale
    out = out.astype(np.float32)
    high = out.astype(jnp.bfloat16)
    low = (out - high.astype(np.float32)).astype(jnp.bfloat16)
    return np.concatenate([high, low], axis=1)


def split(value):
    high = value.astype(BF16)
    return high, (value - high.astype(F32)).astype(BF16)


def sixteen(x):
    c1, c2, c3 = (math.cos(k * math.pi / 8) for k in (1, 2, 3))
    a = [x[n] + x[n + 8] for n in range(8)]
    b = [x[n] - x[n + 8] for n in range(8)]
    c = [a[n] + a[n + 4] for n in range(4)]
    d = [a[n] - a[n + 4] for n in range(4)]
    c02, c13 = c[0] + c[2], c[1] + c[3]
    y = {0: (c02 + c13, None), 8: (c02 - c13, None), 4: (c[0] - c[2], c[3] - c[1])}
    dm, dp = (d[1] - d[3]) * c2, (d[1] + d[3]) * c2
    y[2] = (d[0] + dm, -(d[2] + dp))
    y[6] = (d[0] - dm, d[2] - dp)
    e = [None] + [b[n] - b[8 - n] for n in (1, 2, 3)]
    g = [None] + [b[n] + b[8 - n] for n in (1, 2, 3)]
    e2, g2 = e[2] * c2, g[2] * c2
    p, q = b[0] + e2, b[0] - e2
    s, t = e[1] * c1 + e[3] * c3, e[1] * c3 - e[3] * c1
    v, w = b[4] + g2, g2 - b[4]
    h, k = g[1] * c3 + g[3] * c1, g[1] * c1 - g[3] * c3
    y[1] = (p + s, -(v + h))
    y[7] = (p - s, v - h)
    y[3] = (q + t, -(k + w))
    y[5] = (q - t, w - k)
    return y


def contract(a, b):
    return lax.dot_general(a, b, (((1,), (1,)), ((), ())), preferred_element_type=F32)


MESH = pl.DeviceIdType.MESH
GROUPS = ((0, 1), (1, 2), (3, 2), (5, 2), (7, 1))
DEVICES = 128


def place():
    inp, tm = lax.axis_index("inp"), lax.axis_index("tm")
    return inp, tm, (lax.rem(inp // 4, 4), inp // 16 * 2 + tm // 2, lax.rem(inp, 4), lax.rem(tm, 2))


def partner(here, step):
    x, y, z, core = here
    k = lax.rem(step * 37, DEVICES)
    core = lax.rem(core + k, 2)
    x = lax.rem(x + k // 2, 4)
    y = lax.rem(y + k // 8, 4)
    z = lax.rem(z + k // 32, 4)
    return y // 2 * 16 + x * 4 + z, lax.rem(y, 2) * 2 + core


def kernel(volt, taps, table, out, ext, tapb, xs, send, recv, load_sem, halo_sem, send_sem, recv_sem):
    inputs, frames = volt.shape[0], volt.shape[1]
    blocks = volt.shape[2] // LANES
    inp, tm, here = place()
    me = inp * 4 + tm

    barrier = pltpu.get_barrier_semaphore()
    loads = []
    for l in range(blocks):
        lanes = pl.ds(l * LANES, LANES)
        loads.append(pltpu.make_async_copy(volt.at[:, :, lanes], ext.at[:, l, pl.ds(8, frames), :], load_sem.at[l]))
        loads[-1].start()

    @pl.loop(1, DEVICES)
    def _(k):
        other = lax.rem(me + k, DEVICES)
        pl.semaphore_signal(barrier, inc=1, device_id=(other // 4, lax.rem(other, 4)), device_id_type=MESH)

    for k in range(4):
        for l in range(blocks):
            tapb[k, l] = jnp.broadcast_to(taps[k : k + 1, l * LANES : (l + 1) * LANES], (8, LANES))
    for load in loads:
        load.wait()
    pl.semaphore_wait(barrier, DEVICES - 1)

    halo = pltpu.make_async_remote_copy(
        src_ref=ext.at[:, :, pl.ds(5 + frames, 3), :],
        dst_ref=ext.at[:, :, pl.ds(5, 3), :],
        send_sem=halo_sem.at[0],
        recv_sem=halo_sem.at[1],
        device_id=(inp, lax.rem(tm + 1, 4)),
        device_id_type=MESH,
    )

    @pl.when(tm < 3)
    def _():
        halo.start()

    step = 16

    def filtered(i, f):
        parts = []
        for l in range(blocks):
            halves = []
            for j in range(step // 8):
                row = 5 + f * step + j * 8
                acc = tapb[0, l] * ext[i, l, pl.ds(row, 8), :]
                for k in range(1, 4):
                    acc = acc + tapb[k, l] * ext[i, l, pl.ds(row + k, 8), :]
                halves.append(acc)
            parts.append(jnp.concatenate(halves, axis=0))
        y = sixteen(parts)
        rows = pl.ds(pl.multiple_of(i * frames, frames) + f * step, step)
        for r in range(9):
            real, imag = y[r]
            high, low = split(real)
            xs[r, 0, 0, rows, :] = high
            xs[r, 1, 0, rows, :] = low
            xs[r, 0, 1, rows, :] = -high
            xs[r, 1, 1, rows, :] = -low
            if imag is not None:
                high, low = split(imag)
                xs[r, 0, 2, rows, :] = high
                xs[r, 1, 2, rows, :] = low

    @pl.loop(0, inputs)
    def _(i):
        for f in range(1, frames // step):
            filtered(i, f)

    @pl.when(tm > 0)
    def _():
        halo.wait_recv()

    @pl.when(tm == 0)
    def _():
        @pl.loop(0, inputs)
        def _(i):
            for l in range(blocks):
                ext[i, l, 5:8, :] = jnp.zeros((3, LANES), F32)

    @pl.loop(0, inputs)
    def _(i):
        filtered(i, 0)

    @pl.when(tm < 3)
    def _():
        halo.wait_send()

    def operand(r, part, pair):
        rows_ = []
        for i in (2 * pair, 2 * pair + 1):
            rows = pl.ds(i * frames, frames)
            real, minus = xs[r, part, 0, rows, :], xs[r, part, 1, rows, :]
            imag = jnp.zeros_like(real) if r in (0, 8) else xs[r, part, 2, rows, :]
            rows_.append(jnp.concatenate([real, imag], axis=1))
            rows_.append(jnp.concatenate([imag, minus], axis=1))
        return jnp.concatenate(rows_, axis=0)

    def product(r, pair):
        both = contract(table[r], operand(r, 0, pair))
        return both[:128] + both[128:] + contract(table[r, 0:128], operand(r, 1, pair))

    flat = send.reshape(DEVICES * 64, LANES)
    for g, (first, count) in enumerate(GROUPS):
        for r in range(first, first + count):
            for pair in range(inputs // 2):
                value = product(r, pair)
                if r == 0:
                    value = value + product(8, pair)
                for h in range(2):
                    flat[pl.ds(r * inputs + 2 * pair + h, DEVICES, stride=64), :] = value[:, h * LANES : (h + 1) * LANES]
        slots = pl.ds(first, count)
        target = recv.at[slots, tm, pl.ds(pl.multiple_of(inp * 8, 8), 8), :]
        pltpu.make_async_copy(send.at[me, slots], target, recv_sem.at[g]).start()

        @pl.loop(1, DEVICES)
        def _(k):
            to_inp, to_tm = partner(here, k)
            pltpu.make_async_remote_copy(
                src_ref=send.at[to_inp * 4 + to_tm, slots],
                dst_ref=target,
                send_sem=send_sem,
                recv_sem=recv_sem.at[g],
                device_id=(to_inp, to_tm),
                device_id_type=MESH,
            ).start()

    lane = lax.broadcasted_iota(jnp.int32, (256, LANES), 1)
    sign = jnp.where(lane < 64, 1.0, -1.0).astype(F32)
    odd = lax.rem(tm, 2)
    for g, (first, count) in enumerate(GROUPS):
        slots = recv.at[pl.ds(first, count)]
        pltpu.make_async_copy(slots, slots, recv_sem.at[g]).wait()
        for r in range(first, first + count):
            blocks_, turns = [], []
            for t in range(4):
                block = recv[r, t]
                blocks_.append(split(block))
                turns.append(split(pltpu.roll(block, 64, 1) * sign))
            ph, plo, th, tlo = (jnp.concatenate([b[part] for b in of], axis=1) for of in (blocks_, turns) for part in (0, 1))
            real = contract(ph, ph) + contract(ph, plo) + contract(plo, ph)
            imag = contract(th, ph) + contract(th, plo) + contract(tlo, ph)
            flip = 1.0 if r == 0 else jnp.where(odd == 1, -1.0, 1.0).astype(F32)
            chan = jnp.where(odd == 1, (8 - r) % 8, r)
            out[0, chan] = real
            out[1, chan] = imag * flip
    sent = send.at[pl.ds(0, DEVICES - 1)]
    pltpu.make_async_copy(sent, sent, send_sem).wait()


def on_device(voltages, taps):
    inputs, frames, nfft = voltages.shape
    table = jnp.asarray(tables(nfft, 4 * frames))
    vmem = pl.BlockSpec(memory_space=pltpu.VMEM)
    return pl.pallas_call(
        kernel,
        out_shape=jax.ShapeDtypeStruct((2, 8, 256, 256), F32),
        in_specs=[pl.BlockSpec(memory_space=pl.ANY), vmem, vmem],
        out_specs=vmem,
        scratch_shapes=[
            pltpu.VMEM((inputs, nfft // LANES, frames + 8, LANES), F32),
            pltpu.VMEM((4, nfft // LANES, 8, LANES), F32),
            pltpu.VMEM((9, 2, 3, inputs * frames, LANES), BF16),
            pltpu.VMEM((DEVICES, 8, inputs, LANES), F32),
            pltpu.VMEM((8, 4, 256, LANES), F32),
            pltpu.SemaphoreType.DMA((nfft // LANES,)),
            pltpu.SemaphoreType.DMA((2,)),
            pltpu.SemaphoreType.DMA,
            pltpu.SemaphoreType.DMA((len(GROUPS),)),
        ],
        compiler_params=pltpu.CompilerParams(collective_id=0, has_side_effects=True, vmem_limit_bytes=40 << 20),
    )(voltages, taps, table)


def solution(mesh):
    return jax.shard_map(
        on_device,
        mesh=mesh,
        in_specs=(P("inp", "tm", None), P()),
        out_specs=P(None, ("inp", "tm"), None, None),
        check_vma=False,
    )
```

```python
import functools
import math

import jax
import jax.numpy as jnp
import numpy as np
from jax import lax
from jax.experimental import pallas as pl
from jax.experimental.pallas import tpu as pltpu
from jax.sharding import PartitionSpec as P

LANES = 128
F32 = jnp.float32
BF16 = jnp.bfloat16


def tables(nfft, spectra):
    dests = 128
    n2 = np.arange(LANES)
    scale = 1.0 / math.sqrt(nfft) / math.sqrt(spectra)
    out = np.zeros((9, dests, 2 * LANES), np.float64)
    for r in range(9):
        for m in range(dests):
            if (r == 0 and m % 2 == 1) or (r == 8 and m % 2 == 0):
                continue
            q = m // 2 if (m % 2 == 0 or r == 8) else 127 - m // 2
            angle = 2.0 * np.pi * ((n2 * (16 * q + r)) % nfft) / nfft
            out[r, m, :LANES] = np.cos(angle) * scale
            out[r, m, LANES:] = np.sin(angle) * scale
    out = out.astype(np.float32)
    high = out.astype(jnp.bfloat16)
    low = (out - high.astype(np.float32)).astype(jnp.bfloat16)
    return np.concatenate([high, low], axis=1)


def split(value):
    high = value.astype(BF16)
    return high, (value - high.astype(F32)).astype(BF16)


def sixteen(x):
    c1, c2, c3 = (math.cos(k * math.pi / 8) for k in (1, 2, 3))
    a = [x[n] + x[n + 8] for n in range(8)]
    b = [x[n] - x[n + 8] for n in range(8)]
    c = [a[n] + a[n + 4] for n in range(4)]
    d = [a[n] - a[n + 4] for n in range(4)]
    c02, c13 = c[0] + c[2], c[1] + c[3]
    y = {0: (c02 + c13, None), 8: (c02 - c13, None), 4: (c[0] - c[2], c[3] - c[1])}
    dm, dp = (d[1] - d[3]) * c2, (d[1] + d[3]) * c2
    y[2] = (d[0] + dm, -(d[2] + dp))
    y[6] = (d[0] - dm, d[2] - dp)
    e = [None] + [b[n] - b[8 - n] for n in (1, 2, 3)]
    g = [None] + [b[n] + b[8 - n] for n in (1, 2, 3)]
    e2, g2 = e[2] * c2, g[2] * c2
    p, q = b[0] + e2, b[0] - e2
    s, t = e[1] * c1 + e[3] * c3, e[1] * c3 - e[3] * c1
    v, w = b[4] + g2, g2 - b[4]
    h, k = g[1] * c3 + g[3] * c1, g[1] * c1 - g[3] * c3
    y[1] = (p + s, -(v + h))
    y[7] = (p - s, v - h)
    y[3] = (q + t, -(k + w))
    y[5] = (q - t, w - k)
    return y


def contract(a, b):
    return lax.dot_general(a, b, (((1,), (1,)), ((), ())), preferred_element_type=F32)


MESH = pl.DeviceIdType.MESH
GROUPS = ((0, 2), (2, 2), (4, 2), (6, 1), (7, 1))
DEVICES = 128


def place():
    inp, tm = lax.axis_index("inp"), lax.axis_index("tm")
    return inp, tm, (lax.rem(inp // 4, 4), inp // 16 * 2 + tm // 2, lax.rem(inp, 4), lax.rem(tm, 2))


def partner(here, step):
    x, y, z, core = here
    k = lax.rem(step * 37, DEVICES)
    core = lax.rem(core + k, 2)
    x = lax.rem(x + k // 2, 4)
    y = lax.rem(y + k // 8, 4)
    z = lax.rem(z + k // 32, 4)
    return y // 2 * 16 + x * 4 + z, lax.rem(y, 2) * 2 + core


def kernel(volt, taps_hbm, table_hbm, out, taps, table, ext, tapb, xs, send, recv, load_sem, halo_send, halo_recv, line_sem, send_sem, recv_sem):
    inputs, frames = volt.shape[0], volt.shape[1]
    blocks = volt.shape[2] // LANES
    inp, tm, here = place()
    me = inp * 4 + tm

    high, x, z = inp // 16 * 16, lax.rem(inp // 4, 4) * 4, lax.rem(inp, 4)
    line_z = [(high + x + lax.rem(z + k, 4), tm) for k in (1, 2, 3)]
    line_x = [(high + lax.rem(x + 4 * k, 16) + z, tm) for k in (1, 2, 3)]
    line_y = [(lax.rem(inp + 16, 32), tm)]
    line_t = [(inp, lax.rem(tm + k, 4)) for k in (1, 2, 3)]
    lines = (line_z, line_x, line_y)

    def greet(line, sem):
        for device in line:
            pl.semaphore_signal(sem, inc=1, device_id=device, device_id_type=MESH)

    barrier = pltpu.get_barrier_semaphore()
    for line in (line_t, *lines):
        greet(line, barrier)

    loads = [
        pltpu.make_async_copy(taps_hbm, taps, load_sem.at[blocks]),
        pltpu.make_async_copy(table_hbm, table, load_sem.at[blocks + 1]),
    ]
    loads[0].start()
    for l in range(blocks):
        lanes = pl.ds(l * LANES, LANES)
        loads.append(pltpu.make_async_copy(volt.at[:, :, lanes], ext.at[:, l, pl.ds(8, frames), :], load_sem.at[l]))
        loads[-1].start()
    loads[1].start()

    pl.semaphore_wait(barrier, 10)
    halos = [
        pltpu.make_async_remote_copy(
            src_ref=volt.at[:, pl.ds(frames - 3, 3), pl.ds(l * LANES, LANES)],
            dst_ref=ext.at[:, l, pl.ds(5, 3), :],
            send_sem=halo_send.at[l],
            recv_sem=halo_recv.at[l],
            device_id=(inp, lax.rem(tm + 1, 4)),
            device_id_type=MESH,
        )
        for l in range(blocks)
    ]

    @pl.when(tm < 3)
    def _():
        for halo in halos:
            halo.start()

    greet(line_z, line_sem.at[0])

    @pl.when(tm == 0)
    def _():
        @pl.loop(0, inputs)
        def _(i):
            for l in range(blocks):
                ext[i, l, 5:8, :] = jnp.zeros((3, LANES), F32)

    loads[0].wait()
    for k in range(4):
        for l in range(blocks):
            tapb[k, l] = jnp.broadcast_to(taps[k : k + 1, l * LANES : (l + 1) * LANES], (8, LANES))
    for load in loads[2:]:
        load.wait()

    step = 16

    def filtered(i, f):
        parts = []
        for l in range(blocks):
            halves = []
            for j in range(step // 8):
                row = 5 + f * step + j * 8
                acc = tapb[0, l] * ext[i, l, pl.ds(row, 8), :]
                for k in range(1, 4):
                    acc = acc + tapb[k, l] * ext[i, l, pl.ds(row + k, 8), :]
                halves.append(acc)
            parts.append(jnp.concatenate(halves, axis=0))
        y = sixteen(parts)
        rows = pl.ds(pl.multiple_of(i * frames, frames) + f * step, step)
        for r in range(9):
            real, imag = y[r]
            high, low = split(real)
            xs[r, 0, 0, rows, :] = high
            xs[r, 1, 0, rows, :] = low
            xs[r, 0, 1, rows, :] = -high
            xs[r, 1, 1, rows, :] = -low
            if imag is not None:
                high, low = split(imag)
                xs[r, 0, 2, rows, :] = high
                xs[r, 1, 2, rows, :] = low

    def later(first, last):
        @pl.loop(first, last)
        def _(i):
            for f in range(1, frames // step):
                filtered(i, f)

    later(0, 2)
    pl.semaphore_wait(line_sem.at[0], 3)
    greet(line_x, line_sem.at[1])
    later(2, 5)
    pl.semaphore_wait(line_sem.at[1], 3)
    greet(line_y, line_sem.at[2])
    later(5, inputs)

    @pl.when(tm > 0)
    def _():
        for halo in halos:
            halo.wait_recv()

    @pl.loop(0, inputs)
    def _(i):
        filtered(i, 0)

    loads[1].wait()
    pl.semaphore_wait(line_sem.at[2], 1)

    def operand(r, part, pair):
        rows_ = []
        for i in (2 * pair, 2 * pair + 1):
            rows = pl.ds(i * frames, frames)
            real, minus = xs[r, part, 0, rows, :], xs[r, part, 1, rows, :]
            imag = jnp.zeros_like(real) if r in (0, 8) else xs[r, part, 2, rows, :]
            rows_.append(jnp.concatenate([real, imag], axis=1))
            rows_.append(jnp.concatenate([imag, minus], axis=1))
        return jnp.concatenate(rows_, axis=0)

    def product(r, pair):
        both = contract(table[r], operand(r, 0, pair))
        return both[:128] + both[128:] + contract(table[r, 0:128], operand(r, 1, pair))

    flat = send.reshape(DEVICES * 64, LANES)
    for g, (first, count) in enumerate(GROUPS):
        for r in range(first, first + count):
            for pair in range(inputs // 2):
                value = product(r, pair)
                if r == 0:
                    value = value + product(8, pair)
                for h in range(2):
                    flat[pl.ds(r * inputs + 2 * pair + h, DEVICES, stride=64), :] = value[:, h * LANES : (h + 1) * LANES]
        slots = pl.ds(first, count)
        target = recv.at[slots, tm, pl.ds(pl.multiple_of(inp * 8, 8), 8), :]
        pltpu.make_async_copy(send.at[me, slots], target, recv_sem.at[g]).start()

        @pl.loop(1, DEVICES)
        def _(k):
            to_inp, to_tm = partner(here, k)
            pltpu.make_async_remote_copy(
                src_ref=send.at[to_inp * 4 + to_tm, slots],
                dst_ref=target,
                send_sem=send_sem,
                recv_sem=recv_sem.at[g],
                device_id=(to_inp, to_tm),
                device_id_type=MESH,
            ).start()

    lane = lax.broadcasted_iota(jnp.int32, (256, LANES), 1)
    sign = jnp.where(lane < 64, 1.0, -1.0).astype(F32)
    odd = lax.rem(tm, 2)
    for g, (first, count) in enumerate(GROUPS):
        slots = recv.at[pl.ds(first, count)]
        pltpu.make_async_copy(slots, slots, recv_sem.at[g]).wait()
        for r in range(first, first + count):
            blocks_, turns = [], []
            for t in range(4):
                block = recv[r, t]
                blocks_.append(split(block))
                turns.append(split(pltpu.roll(block, 64, 1) * sign))
            ph, plo, th, tlo = (jnp.concatenate([b[part] for b in of], axis=1) for of in (blocks_, turns) for part in (0, 1))
            real = contract(ph, ph) + contract(ph, plo) + contract(plo, ph)
            imag = contract(th, ph) + contract(th, plo) + contract(tlo, ph)
            flip = 1.0 if r == 0 else jnp.where(odd == 1, -1.0, 1.0).astype(F32)
            chan = jnp.where(odd == 1, (8 - r) % 8, r)
            out[0, chan] = real
            out[1, chan] = imag * flip

    @pl.when(tm < 3)
    def _():
        for halo in halos:
            halo.wait_send()

    sent = send.at[pl.ds(0, DEVICES - 1)]
    pltpu.make_async_copy(sent, sent, send_sem).wait()


def on_device(voltages, taps):
    inputs, frames, nfft = voltages.shape
    table = jnp.asarray(tables(nfft, 4 * frames))
    vmem = pl.BlockSpec(memory_space=pltpu.VMEM)
    hbm = pl.BlockSpec(memory_space=pltpu.HBM)
    return pl.pallas_call(
        kernel,
        out_shape=jax.ShapeDtypeStruct((2, 8, 256, 256), F32),
        in_specs=[hbm, hbm, hbm],
        out_specs=vmem,
        scratch_shapes=[
            pltpu.VMEM(taps.shape, F32),
            pltpu.VMEM(table.shape, BF16),
            pltpu.VMEM((inputs, nfft // LANES, frames + 8, LANES), F32),
            pltpu.VMEM((4, nfft // LANES, 8, LANES), F32),
            pltpu.VMEM((9, 2, 3, inputs * frames, LANES), BF16),
            pltpu.VMEM((DEVICES, 8, inputs, LANES), F32),
            pltpu.VMEM((8, 4, 256, LANES), F32),
            pltpu.SemaphoreType.DMA((nfft // LANES + 2,)),
            pltpu.SemaphoreType.DMA((nfft // LANES,)),
            pltpu.SemaphoreType.DMA((nfft // LANES,)),
            pltpu.SemaphoreType.REGULAR((3,)),
            pltpu.SemaphoreType.DMA,
            pltpu.SemaphoreType.DMA((len(GROUPS),)),
        ],
        compiler_params=pltpu.CompilerParams(collective_id=0, has_side_effects=True, vmem_limit_bytes=40 << 20),
    )(*(pltpu.with_memory_space_constraint(v, pltpu.HBM) for v in (voltages, taps, table)))


def solution(mesh):
    return jax.shard_map(
        on_device,
        mesh=mesh,
        in_specs=(P("inp", "tm", None), P()),
        out_specs=P(None, ("inp", "tm"), None, None),
        check_vma=False,
    )
```

```python
import functools
import math

import jax
import jax.numpy as jnp
import numpy as np
from jax import lax
from jax.experimental import pallas as pl
from jax.experimental.pallas import tpu as pltpu
from jax.sharding import PartitionSpec as P

LANES = 128
F32 = jnp.float32
BF16 = jnp.bfloat16


def tables(nfft, spectra):
    dests = 128
    n2 = np.arange(LANES)
    scale = 1.0 / math.sqrt(nfft) / math.sqrt(spectra)
    out = np.zeros((9, dests, 2 * LANES), np.float64)
    for r in range(9):
        for m in range(dests):
            if (r == 0 and m % 2 == 1) or (r == 8 and m % 2 == 0):
                continue
            q = m // 2 if (m % 2 == 0 or r == 8) else 127 - m // 2
            angle = 2.0 * np.pi * ((n2 * (16 * q + r)) % nfft) / nfft
            out[r, m, :LANES] = np.cos(angle) * scale
            out[r, m, LANES:] = np.sin(angle) * scale
    out = out.astype(np.float32)
    high = out.astype(jnp.bfloat16)
    low = (out - high.astype(np.float32)).astype(jnp.bfloat16)
    return np.concatenate([high, low], axis=1)


def split(value):
    high = value.astype(BF16)
    return high, (value - high.astype(F32)).astype(BF16)


def sixteen(x):
    c1, c2, c3 = (math.cos(k * math.pi / 8) for k in (1, 2, 3))
    a = [x[n] + x[n + 8] for n in range(8)]
    b = [x[n] - x[n + 8] for n in range(8)]
    c = [a[n] + a[n + 4] for n in range(4)]
    d = [a[n] - a[n + 4] for n in range(4)]
    c02, c13 = c[0] + c[2], c[1] + c[3]
    y = {0: (c02 + c13, None), 8: (c02 - c13, None), 4: (c[0] - c[2], c[3] - c[1])}
    dm, dp = (d[1] - d[3]) * c2, (d[1] + d[3]) * c2
    y[2] = (d[0] + dm, -(d[2] + dp))
    y[6] = (d[0] - dm, d[2] - dp)
    e = [None] + [b[n] - b[8 - n] for n in (1, 2, 3)]
    g = [None] + [b[n] + b[8 - n] for n in (1, 2, 3)]
    e2, g2 = e[2] * c2, g[2] * c2
    p, q = b[0] + e2, b[0] - e2
    s, t = e[1] * c1 + e[3] * c3, e[1] * c3 - e[3] * c1
    v, w = b[4] + g2, g2 - b[4]
    h, k = g[1] * c3 + g[3] * c1, g[1] * c1 - g[3] * c3
    y[1] = (p + s, -(v + h))
    y[7] = (p - s, v - h)
    y[3] = (q + t, -(k + w))
    y[5] = (q - t, w - k)
    return y


def contract(a, b):
    return lax.dot_general(a, b, (((1,), (1,)), ((), ())), preferred_element_type=F32)


MESH = pl.DeviceIdType.MESH
GROUPS = ((0, 2), (2, 2), (4, 2), (6, 1), (7, 1))
DEVICES = 128


def place():
    inp, tm = lax.axis_index("inp"), lax.axis_index("tm")
    return inp, tm, (lax.rem(inp // 4, 4), inp // 16 * 2 + tm // 2, lax.rem(inp, 4), lax.rem(tm, 2))


def offsets():
    shuffled = np.random.RandomState(1).permutation(np.arange(1, DEVICES))
    steps = [(int(k) // 2 % 4, int(k) // 8 % 4, int(k) // 32, int(k) % 2) for k in shuffled]
    return sorted(steps, key=lambda step: -sum(min(d, 4 - d) for d in step[:3]))


def visibility(blocks, r, tm):
    odd = lax.rem(tm, 2)
    lane = lax.broadcasted_iota(jnp.int32, (256, LANES), 1)
    sign = jnp.where(lane < 64, 1.0, -1.0).astype(F32)
    plain = [split(b) for b in blocks]
    turned = [split(pltpu.roll(b, 64, 1) * sign) for b in blocks]
    ph, plo, th, tlo = (jnp.concatenate([b[part] for b in of], axis=1) for of in (plain, turned) for part in (0, 1))
    real = contract(ph, ph) + contract(ph, plo) + contract(plo, ph)
    imag = contract(th, ph) + contract(th, plo) + contract(tlo, ph)
    flip = 1.0 if r == 0 else jnp.where(odd == 1, -1.0, 1.0).astype(F32)
    return jnp.where(odd == 1, (8 - r) % 8, r), real, imag * flip


def tail_kernel(begun, last, out, stage, sem):
    tm = lax.axis_index("tm")
    final = jnp.where(lax.rem(tm, 2) == 1, 1, 7)
    writes = []
    for k in range(1, 8):
        chan = lax.rem(final + k, 8)
        writes.append(pltpu.make_async_copy(begun.at[:, chan], out.at[:, chan], sem.at[k]))
        writes[-1].start()
    chan, real, imag = visibility([last[0, t] for t in range(4)], 7, tm)
    stage[0] = real
    stage[1] = imag
    writes.append(pltpu.make_async_copy(stage, out.at[:, chan], sem.at[0]))
    writes[-1].start()
    for write in writes:
        write.wait()


def kernel(volt, taps_hbm, table_hbm, out, last, taps, table, ext, tapb, xs, send, recv, load_sem, halo_send, halo_recv, column_sem, send_sem, recv_sem):
    inputs, frames = volt.shape[0], volt.shape[1]
    blocks = volt.shape[2] // LANES
    inp, tm, here = place()
    me = inp * 4 + tm

    high, low = inp // 16 * 16, lax.rem(inp, 16)
    plane = [(high + lax.rem(low + k, 16), tm) for k in range(1, 16)]
    column = [(inp, lax.rem(tm + k, 4)) for k in (1, 2, 3)] + [(lax.rem(inp + 16, 32), lax.rem(tm + k, 4)) for k in range(4)]

    def greet(line, sem):
        for device in line:
            pl.semaphore_signal(sem, inc=1, device_id=device, device_id_type=MESH)

    barrier = pltpu.get_barrier_semaphore()
    greet(column, barrier)
    greet(plane, barrier)

    loads = [
        pltpu.make_async_copy(taps_hbm, taps, load_sem.at[blocks]),
        pltpu.make_async_copy(table_hbm, table, load_sem.at[blocks + 1]),
    ]
    loads[0].start()
    for l in range(blocks):
        lanes = pl.ds(l * LANES, LANES)
        loads.append(pltpu.make_async_copy(volt.at[:, :, lanes], ext.at[:, l, pl.ds(8, frames), :], load_sem.at[l]))
        loads[-1].start()
    loads[1].start()

    pl.semaphore_wait(barrier, 22)
    greet(column, column_sem)
    halos = [
        pltpu.make_async_remote_copy(
            src_ref=volt.at[:, pl.ds(frames - 3, 3), pl.ds(l * LANES, LANES)],
            dst_ref=ext.at[:, l, pl.ds(5, 3), :],
            send_sem=halo_send.at[l],
            recv_sem=halo_recv.at[l],
            device_id=(inp, lax.rem(tm + 1, 4)),
            device_id_type=MESH,
        )
        for l in range(blocks)
    ]

    @pl.when(tm < 3)
    def _():
        for halo in halos:
            halo.start()

    @pl.when(tm == 0)
    def _():
        @pl.loop(0, inputs)
        def _(i):
            for l in range(blocks):
                ext[i, l, 5:8, :] = jnp.zeros((3, LANES), F32)

    loads[0].wait()
    for k in range(4):
        for l in range(blocks):
            tapb[k, l] = jnp.broadcast_to(taps[k : k + 1, l * LANES : (l + 1) * LANES], (8, LANES))
    for load in loads[2:]:
        load.wait()

    step = 16

    def filtered(i, f):
        parts = []
        for l in range(blocks):
            halves = []
            for j in range(step // 8):
                row = 5 + f * step + j * 8
                acc = tapb[0, l] * ext[i, l, pl.ds(row, 8), :]
                for k in range(1, 4):
                    acc = acc + tapb[k, l] * ext[i, l, pl.ds(row + k, 8), :]
                halves.append(acc)
            parts.append(jnp.concatenate(halves, axis=0))
        y = sixteen(parts)
        rows = pl.ds(pl.multiple_of(i * frames, frames) + f * step, step)
        for r in range(9):
            real, imag = y[r]
            high, low = split(real)
            xs[r, 0, 0, rows, :] = high
            xs[r, 1, 0, rows, :] = low
            xs[r, 0, 1, rows, :] = -high
            xs[r, 1, 1, rows, :] = -low
            if imag is not None:
                high, low = split(imag)
                xs[r, 0, 2, rows, :] = high
                xs[r, 1, 2, rows, :] = low

    def later(first, last):
        @pl.loop(first, last)
        def _(i):
            for f in range(1, frames // step):
                filtered(i, f)

    later(0, inputs)

    @pl.when(tm > 0)
    def _():
        for halo in halos:
            halo.wait_recv()

    @pl.loop(0, inputs)
    def _(i):
        filtered(i, 0)

    loads[1].wait()
    pl.semaphore_wait(column_sem, 7)

    def operand(r, part, pair):
        rows_ = []
        for i in (2 * pair, 2 * pair + 1):
            rows = pl.ds(i * frames, frames)
            real, minus = xs[r, part, 0, rows, :], xs[r, part, 1, rows, :]
            imag = jnp.zeros_like(real) if r in (0, 8) else xs[r, part, 2, rows, :]
            rows_.append(jnp.concatenate([real, imag], axis=1))
            rows_.append(jnp.concatenate([imag, minus], axis=1))
        return jnp.concatenate(rows_, axis=0)

    def product(r, pair):
        both = contract(table[r], operand(r, 0, pair))
        return both[:128] + both[128:] + contract(table[r, 0:128], operand(r, 1, pair))

    flat = send.reshape(DEVICES * 64, LANES)

    def fill(r):
        for pair in range(inputs // 2):
            value = product(r, pair)
            if r == 0:
                value = value + product(8, pair)
            for h in range(2):
                flat[pl.ds(r * inputs + 2 * pair + h, DEVICES, stride=64), :] = value[:, h * LANES : (h + 1) * LANES]

    rows = pl.ds(pl.multiple_of(inp * 8, 8), 8)

    def landing(first, count):
        return last.at[pl.ds(0, 1), tm, rows, :] if first == 7 else recv.at[pl.ds(first, count), tm, rows, :]

    def ship(g, to_inp, to_tm):
        first, count = GROUPS[g]
        pltpu.make_async_remote_copy(
            src_ref=send.at[to_inp * 4 + to_tm, pl.ds(first, count)],
            dst_ref=landing(first, count),
            send_sem=send_sem,
            recv_sem=recv_sem.at[g],
            device_id=(to_inp, to_tm),
            device_id_type=MESH,
        ).start()

    x, y, z, core = here
    x_at = [lax.rem(x + j, 4) * 4 for j in range(4)]
    y_at = [lax.rem(y + j, 4) for j in range(4)]
    y_at = [(at // 2 * 16, lax.rem(at, 2) * 2) for at in y_at]
    z_at = [lax.rem(z + j, 4) for j in range(4)]
    core_at = [core, 1 - core]

    def exchange(g):
        first, count = GROUPS[g]
        pltpu.make_async_copy(send.at[me, pl.ds(first, count)], landing(first, count), recv_sem.at[g]).start()
        for dx, dy, dz, dc in offsets():
            ship(g, y_at[dy][0] + x_at[dx] + z_at[dz], y_at[dy][1] + core_at[dc])

    for g, (first, count) in enumerate(GROUPS):
        for r in range(first, first + count):
            fill(r)
        exchange(g)

    for g, (first, count) in enumerate(GROUPS[:-1]):
        slots = recv.at[pl.ds(first, count)]
        pltpu.make_async_copy(slots, slots, recv_sem.at[g]).wait()
        for r in range(first, first + count):
            chan, real, imag = visibility([recv[r, t] for t in range(4)], r, tm)
            out[0, chan] = real
            out[1, chan] = imag
    pltpu.make_async_copy(last, last, recv_sem.at[len(GROUPS) - 1]).wait()
    @pl.when(tm < 3)
    def _():
        for halo in halos:
            halo.wait_send()

    sent = send.at[pl.ds(0, DEVICES - 1)]
    pltpu.make_async_copy(sent, sent, send_sem).wait()


def on_device(voltages, taps):
    inputs, frames, nfft = voltages.shape
    table = jnp.asarray(tables(nfft, 4 * frames))
    vmem = pl.BlockSpec(memory_space=pltpu.VMEM)
    hbm = pl.BlockSpec(memory_space=pltpu.HBM)
    result = jax.ShapeDtypeStruct((2, 8, 256, 256), F32)
    begun, last = pl.pallas_call(
        kernel,
        out_shape=(result, jax.ShapeDtypeStruct((1, 4, 256, LANES), F32)),
        in_specs=[hbm, hbm, hbm],
        out_specs=(vmem, vmem),
        scratch_shapes=[
            pltpu.VMEM(taps.shape, F32),
            pltpu.VMEM(table.shape, BF16),
            pltpu.VMEM((inputs, nfft // LANES, frames + 8, LANES), F32),
            pltpu.VMEM((4, nfft // LANES, 8, LANES), F32),
            pltpu.VMEM((9, 2, 3, inputs * frames, LANES), BF16),
            pltpu.VMEM((DEVICES, 8, inputs, LANES), F32),
            pltpu.VMEM((7, 4, 256, LANES), F32),
            pltpu.SemaphoreType.DMA((nfft // LANES + 2,)),
            pltpu.SemaphoreType.DMA((nfft // LANES,)),
            pltpu.SemaphoreType.DMA((nfft // LANES,)),
            pltpu.SemaphoreType.REGULAR,
            pltpu.SemaphoreType.DMA,
            pltpu.SemaphoreType.DMA((len(GROUPS),)),
        ],
        compiler_params=pltpu.CompilerParams(collective_id=0, has_side_effects=True, vmem_limit_bytes=40 << 20),
    )(*(pltpu.with_memory_space_constraint(v, pltpu.HBM) for v in (voltages, taps, table)))
    return pl.pallas_call(
        tail_kernel,
        out_shape=result,
        in_specs=[vmem, vmem],
        out_specs=hbm,
        scratch_shapes=[pltpu.VMEM((2, 256, 256), F32), pltpu.SemaphoreType.DMA((8,))],
        compiler_params=pltpu.CompilerParams(vmem_limit_bytes=24 << 20),
    )(begun, last)


def solution(mesh):
    return jax.shard_map(
        on_device,
        mesh=mesh,
        in_specs=(P("inp", "tm", None), P()),
        out_specs=P(None, ("inp", "tm"), None, None),
        check_vma=False,
    )
```

```python
import functools
import math

import jax
import jax.numpy as jnp
import numpy as np
from jax import lax
from jax.experimental import pallas as pl
from jax.experimental.pallas import tpu as pltpu
from jax.sharding import PartitionSpec as P

LANES = 128
F32 = jnp.float32
BF16 = jnp.bfloat16


def tables(nfft, spectra):
    dests = 128
    n2 = np.arange(LANES)
    scale = 1.0 / math.sqrt(nfft) / math.sqrt(spectra)
    out = np.zeros((9, dests, 2 * LANES), np.float64)
    for r in range(9):
        for m in range(dests):
            if (r == 0 and m % 2 == 1) or (r == 8 and m % 2 == 0):
                continue
            q = m // 2 if (m % 2 == 0 or r == 8) else 127 - m // 2
            angle = 2.0 * np.pi * ((n2 * (16 * q + r)) % nfft) / nfft
            out[r, m, :LANES] = np.cos(angle) * scale
            out[r, m, LANES:] = np.sin(angle) * scale
    out = out.astype(np.float32)
    high = out.astype(jnp.bfloat16)
    low = (out - high.astype(np.float32)).astype(jnp.bfloat16)
    return np.concatenate([high, low], axis=1)


def split(value):
    high = value.astype(BF16)
    return high, (value - high.astype(F32)).astype(BF16)


def sixteen(x):
    c1, c2, c3 = (math.cos(k * math.pi / 8) for k in (1, 2, 3))
    a = [x[n] + x[n + 8] for n in range(8)]
    b = [x[n] - x[n + 8] for n in range(8)]
    c = [a[n] + a[n + 4] for n in range(4)]
    d = [a[n] - a[n + 4] for n in range(4)]
    c02, c13 = c[0] + c[2], c[1] + c[3]
    y = {0: (c02 + c13, None), 8: (c02 - c13, None), 4: (c[0] - c[2], c[3] - c[1])}
    dm, dp = (d[1] - d[3]) * c2, (d[1] + d[3]) * c2
    y[2] = (d[0] + dm, -(d[2] + dp))
    y[6] = (d[0] - dm, d[2] - dp)
    e = [None] + [b[n] - b[8 - n] for n in (1, 2, 3)]
    g = [None] + [b[n] + b[8 - n] for n in (1, 2, 3)]
    e2, g2 = e[2] * c2, g[2] * c2
    p, q = b[0] + e2, b[0] - e2
    s, t = e[1] * c1 + e[3] * c3, e[1] * c3 - e[3] * c1
    v, w = b[4] + g2, g2 - b[4]
    h, k = g[1] * c3 + g[3] * c1, g[1] * c1 - g[3] * c3
    y[1] = (p + s, -(v + h))
    y[7] = (p - s, v - h)
    y[3] = (q + t, -(k + w))
    y[5] = (q - t, w - k)
    return y


def contract(a, b):
    return lax.dot_general(a, b, (((1,), (1,)), ((), ())), preferred_element_type=F32)


MESH = pl.DeviceIdType.MESH
GROUPS = ((1, 2), (3, 2), (5, 2), (7, 1), (0, 1))
DEVICES = 128


def place():
    inp, tm = lax.axis_index("inp"), lax.axis_index("tm")
    return inp, tm, (lax.rem(inp // 4, 4), inp // 16 * 2 + tm // 2, lax.rem(inp, 4), lax.rem(tm, 2))


def offsets():
    shuffled = np.random.RandomState(1).permutation(np.arange(1, DEVICES))
    steps = [(int(k) // 2 % 4, int(k) // 8 % 4, int(k) // 32, int(k) % 2) for k in shuffled]
    return sorted(steps, key=lambda step: -sum(min(d, 4 - d) for d in step[:3]))


def visibility(blocks, r, tm):
    odd = lax.rem(tm, 2)
    lane = lax.broadcasted_iota(jnp.int32, (256, LANES), 1)
    sign = jnp.where(lane < 64, 1.0, -1.0).astype(F32)
    plain = [split(b) for b in blocks]
    turned = [split(pltpu.roll(b, 64, 1) * sign) for b in blocks]
    ph, plo, th, tlo = (jnp.concatenate([b[part] for b in of], axis=1) for of in (plain, turned) for part in (0, 1))
    real = contract(ph, ph) + contract(ph, plo) + contract(plo, ph)
    imag = contract(th, ph) + contract(th, plo) + contract(tlo, ph)
    flip = 1.0 if r == 0 else jnp.where(odd == 1, -1.0, 1.0).astype(F32)
    return jnp.where(odd == 1, (8 - r) % 8, r), real, imag * flip


def tail_kernel(begun, last, out, stage, sem):
    tm = lax.axis_index("tm")
    writes = [pltpu.make_async_copy(begun.at[:, pl.ds(1, 7)], out.at[:, pl.ds(1, 7)], sem.at[0])]
    writes[0].start()
    _, real, imag = visibility([last[0, t] for t in range(4)], 0, tm)
    stage[0] = real
    stage[1] = imag
    writes.append(pltpu.make_async_copy(stage, out.at[:, 0], sem.at[1]))
    writes[-1].start()
    for write in writes:
        write.wait()


def kernel(volt, taps_hbm, table_hbm, out, last, taps, table, ext, tapb, xs, send, recv, load_sem, halo_send, halo_recv, column_sem, send_sem, recv_sem):
    inputs, frames = volt.shape[0], volt.shape[1]
    blocks = volt.shape[2] // LANES
    inp, tm, here = place()
    me = inp * 4 + tm

    high, low = inp // 16 * 16, lax.rem(inp, 16)
    plane = [(high + lax.rem(low + k, 16), tm) for k in range(1, 16)]
    column = [(inp, lax.rem(tm + k, 4)) for k in (1, 2, 3)] + [(lax.rem(inp + 16, 32), lax.rem(tm + k, 4)) for k in range(4)]

    def greet(line, sem):
        for device in line:
            pl.semaphore_signal(sem, inc=1, device_id=device, device_id_type=MESH)

    barrier = pltpu.get_barrier_semaphore()
    greet(column, barrier)
    greet(plane, barrier)

    loads = [
        pltpu.make_async_copy(taps_hbm, taps, load_sem.at[blocks]),
        pltpu.make_async_copy(table_hbm, table, load_sem.at[blocks + 1]),
    ]
    loads[0].start()
    for l in range(blocks):
        lanes = pl.ds(l * LANES, LANES)
        loads.append(pltpu.make_async_copy(volt.at[:, :, lanes], ext.at[:, l, pl.ds(8, frames), :], load_sem.at[l]))
        loads[-1].start()
    loads[1].start()

    pl.semaphore_wait(barrier, 22)
    greet(column, column_sem)
    halos = [
        pltpu.make_async_remote_copy(
            src_ref=volt.at[:, pl.ds(frames - 3, 3), pl.ds(l * LANES, LANES)],
            dst_ref=ext.at[:, l, pl.ds(5, 3), :],
            send_sem=halo_send.at[l],
            recv_sem=halo_recv.at[l],
            device_id=(inp, lax.rem(tm + 1, 4)),
            device_id_type=MESH,
        )
        for l in range(blocks)
    ]

    @pl.when(tm < 3)
    def _():
        for halo in halos:
            halo.start()

    @pl.when(tm == 0)
    def _():
        @pl.loop(0, inputs)
        def _(i):
            for l in range(blocks):
                ext[i, l, 5:8, :] = jnp.zeros((3, LANES), F32)

    loads[0].wait()
    for k in range(4):
        for l in range(blocks):
            tapb[k, l] = jnp.broadcast_to(taps[k : k + 1, l * LANES : (l + 1) * LANES], (8, LANES))
    for load in loads[2:]:
        load.wait()

    step = 16

    def filtered(i, f):
        parts = []
        for l in range(blocks):
            halves = []
            for j in range(step // 8):
                row = 5 + f * step + j * 8
                acc = tapb[0, l] * ext[i, l, pl.ds(row, 8), :]
                for k in range(1, 4):
                    acc = acc + tapb[k, l] * ext[i, l, pl.ds(row + k, 8), :]
                halves.append(acc)
            parts.append(jnp.concatenate(halves, axis=0))
        y = sixteen(parts)
        rows = pl.ds(pl.multiple_of(i * frames, frames) + f * step, step)
        for r in range(9):
            real, imag = y[r]
            high, low = split(real)
            xs[r, 0, 0, rows, :] = high
            xs[r, 1, 0, rows, :] = low
            xs[r, 0, 1, rows, :] = -high
            xs[r, 1, 1, rows, :] = -low
            if imag is not None:
                high, low = split(imag)
                xs[r, 0, 2, rows, :] = high
                xs[r, 1, 2, rows, :] = low

    def later(first, last):
        @pl.loop(first, last)
        def _(i):
            for f in range(1, frames // step):
                filtered(i, f)

    later(0, inputs)

    @pl.when(tm > 0)
    def _():
        for halo in halos:
            halo.wait_recv()

    @pl.loop(0, inputs)
    def _(i):
        filtered(i, 0)

    loads[1].wait()

    def operand(r, part, pair):
        rows_ = []
        for i in (2 * pair, 2 * pair + 1):
            rows = pl.ds(i * frames, frames)
            real, minus = xs[r, part, 0, rows, :], xs[r, part, 1, rows, :]
            imag = jnp.zeros_like(real) if r in (0, 8) else xs[r, part, 2, rows, :]
            rows_.append(jnp.concatenate([real, imag], axis=1))
            rows_.append(jnp.concatenate([imag, minus], axis=1))
        return jnp.concatenate(rows_, axis=0)

    def product(r, pair):
        both = contract(table[r], operand(r, 0, pair))
        return both[:128] + both[128:] + contract(table[r, 0:128], operand(r, 1, pair))

    flat = send.reshape(DEVICES * 64, LANES)

    def fill(r):
        for pair in range(inputs // 2):
            value = product(r, pair)
            if r == 0:
                value = value + product(8, pair)
            for h in range(2):
                flat[pl.ds(r * inputs + 2 * pair + h, DEVICES, stride=64), :] = value[:, h * LANES : (h + 1) * LANES]

    rows = pl.ds(pl.multiple_of(inp * 8, 8), 8)

    def landing(first, count):
        return last.at[pl.ds(0, 1), tm, rows, :] if first == 0 else recv.at[pl.ds(first - 1, count), tm, rows, :]

    def ship(g, to_inp, to_tm):
        first, count = GROUPS[g]
        pltpu.make_async_remote_copy(
            src_ref=send.at[to_inp * 4 + to_tm, pl.ds(first, count)],
            dst_ref=landing(first, count),
            send_sem=send_sem,
            recv_sem=recv_sem.at[g],
            device_id=(to_inp, to_tm),
            device_id_type=MESH,
        ).start()

    x, y, z, core = here
    x_at = [lax.rem(x + j, 4) * 4 for j in range(4)]
    y_at = [lax.rem(y + j, 4) for j in range(4)]
    y_at = [(at // 2 * 16, lax.rem(at, 2) * 2) for at in y_at]
    z_at = [lax.rem(z + j, 4) for j in range(4)]
    core_at = [core, 1 - core]

    def exchange(g):
        first, count = GROUPS[g]
        pltpu.make_async_copy(send.at[me, pl.ds(first, count)], landing(first, count), recv_sem.at[g]).start()
        steps = offsets()
        if g == 0:
            steps = [step for step in steps if step[1] == step[3] == 0] + [step for step in steps if step[1] or step[3]]
        for k, (dx, dy, dz, dc) in enumerate(steps):
            if g == 0 and k == 15:
                pl.semaphore_wait(column_sem, 7)
            ship(g, y_at[dy][0] + x_at[dx] + z_at[dz], y_at[dy][1] + core_at[dc])

    for g, (first, count) in enumerate(GROUPS):
        for r in range(first, first + count):
            fill(r)
        exchange(g)

    for g, (first, count) in enumerate(GROUPS[:-1]):
        slots = recv.at[pl.ds(first - 1, count)]
        pltpu.make_async_copy(slots, slots, recv_sem.at[g]).wait()
        for r in range(first, first + count):
            chan, real, imag = visibility([recv[r - 1, t] for t in range(4)], r, tm)
            out[0, chan] = real
            out[1, chan] = imag
    pltpu.make_async_copy(last, last, recv_sem.at[len(GROUPS) - 1]).wait()
    @pl.when(tm < 3)
    def _():
        for halo in halos:
            halo.wait_send()

    sent = send.at[pl.ds(0, DEVICES - 1)]
    pltpu.make_async_copy(sent, sent, send_sem).wait()


def on_device(voltages, taps):
    inputs, frames, nfft = voltages.shape
    table = jnp.asarray(tables(nfft, 4 * frames))
    vmem = pl.BlockSpec(memory_space=pltpu.VMEM)
    hbm = pl.BlockSpec(memory_space=pltpu.HBM)
    result = jax.ShapeDtypeStruct((2, 8, 256, 256), F32)
    begun, last = pl.pallas_call(
        kernel,
        out_shape=(result, jax.ShapeDtypeStruct((1, 4, 256, LANES), F32)),
        in_specs=[hbm, hbm, hbm],
        out_specs=(vmem, vmem),
        scratch_shapes=[
            pltpu.VMEM(taps.shape, F32),
            pltpu.VMEM(table.shape, BF16),
            pltpu.VMEM((inputs, nfft // LANES, frames + 8, LANES), F32),
            pltpu.VMEM((4, nfft // LANES, 8, LANES), F32),
            pltpu.VMEM((9, 2, 3, inputs * frames, LANES), BF16),
            pltpu.VMEM((DEVICES, 8, inputs, LANES), F32),
            pltpu.VMEM((7, 4, 256, LANES), F32),
            pltpu.SemaphoreType.DMA((nfft // LANES + 2,)),
            pltpu.SemaphoreType.DMA((nfft // LANES,)),
            pltpu.SemaphoreType.DMA((nfft // LANES,)),
            pltpu.SemaphoreType.REGULAR,
            pltpu.SemaphoreType.DMA,
            pltpu.SemaphoreType.DMA((len(GROUPS),)),
        ],
        compiler_params=pltpu.CompilerParams(collective_id=0, has_side_effects=True, vmem_limit_bytes=40 << 20),
    )(*(pltpu.with_memory_space_constraint(v, pltpu.HBM) for v in (voltages, taps, table)))
    return pl.pallas_call(
        tail_kernel,
        out_shape=result,
        in_specs=[vmem, vmem],
        out_specs=hbm,
        scratch_shapes=[pltpu.VMEM((2, 256, 256), F32), pltpu.SemaphoreType.DMA((2,))],
        compiler_params=pltpu.CompilerParams(vmem_limit_bytes=24 << 20),
    )(begun, last)


def solution(mesh):
    return jax.shard_map(
        on_device,
        mesh=mesh,
        in_specs=(P("inp", "tm", None), P()),
        out_specs=P(None, ("inp", "tm"), None, None),
        check_vma=False,
    )
```

```python
import functools
import math

import jax
import jax.numpy as jnp
import numpy as np
from jax import lax
from jax.experimental import pallas as pl
from jax.experimental.pallas import tpu as pltpu
from jax.sharding import PartitionSpec as P

LANES = 128
F32 = jnp.float32
BF16 = jnp.bfloat16


def tables(nfft, spectra):
    dests = 128
    n2 = np.arange(LANES)
    scale = 1.0 / math.sqrt(nfft) / math.sqrt(spectra)
    out = np.zeros((9, dests, 2 * LANES), np.float64)
    for r in range(9):
        for m in range(dests):
            if (r == 0 and m % 2 == 1) or (r == 8 and m % 2 == 0):
                continue
            q = m // 2 if (m % 2 == 0 or r == 8) else 127 - m // 2
            angle = 2.0 * np.pi * ((n2 * (16 * q + r)) % nfft) / nfft
            out[r, m, :LANES] = np.cos(angle) * scale
            out[r, m, LANES:] = np.sin(angle) * scale
    out = out.astype(np.float32)
    high = out.astype(jnp.bfloat16)
    low = (out - high.astype(np.float32)).astype(jnp.bfloat16)
    return np.concatenate([high, low], axis=1)


def split(value):
    high = value.astype(BF16)
    return high, (value - high.astype(F32)).astype(BF16)


def sixteen(x):
    c1, c2, c3 = (math.cos(k * math.pi / 8) for k in (1, 2, 3))
    a = [x[n] + x[n + 8] for n in range(8)]
    b = [x[n] - x[n + 8] for n in range(8)]
    c = [a[n] + a[n + 4] for n in range(4)]
    d = [a[n] - a[n + 4] for n in range(4)]
    c02, c13 = c[0] + c[2], c[1] + c[3]
    y = {0: (c02 + c13, None), 8: (c02 - c13, None), 4: (c[0] - c[2], c[3] - c[1])}
    dm, dp = (d[1] - d[3]) * c2, (d[1] + d[3]) * c2
    y[2] = (d[0] + dm, -(d[2] + dp))
    y[6] = (d[0] - dm, d[2] - dp)
    e = [None] + [b[n] - b[8 - n] for n in (1, 2, 3)]
    g = [None] + [b[n] + b[8 - n] for n in (1, 2, 3)]
    e2, g2 = e[2] * c2, g[2] * c2
    p, q = b[0] + e2, b[0] - e2
    s, t = e[1] * c1 + e[3] * c3, e[1] * c3 - e[3] * c1
    v, w = b[4] + g2, g2 - b[4]
    h, k = g[1] * c3 + g[3] * c1, g[1] * c1 - g[3] * c3
    y[1] = (p + s, -(v + h))
    y[7] = (p - s, v - h)
    y[3] = (q + t, -(k + w))
    y[5] = (q - t, w - k)
    return y


def contract(a, b):
    return lax.dot_general(a, b, (((1,), (1,)), ((), ())), preferred_element_type=F32)


MESH = pl.DeviceIdType.MESH
GROUPS = ((1, 1), (2, 2), (4, 2), (6, 2), (0, 1))
DEVICES = 128


def place():
    inp, tm = lax.axis_index("inp"), lax.axis_index("tm")
    return inp, tm, (lax.rem(inp // 4, 4), inp // 16 * 2 + tm // 2, lax.rem(inp, 4), lax.rem(tm, 2))


def offsets():
    shuffled = np.random.RandomState(1).permutation(np.arange(1, DEVICES))
    steps = [(int(k) // 2 % 4, int(k) // 8 % 4, int(k) // 32, int(k) % 2) for k in shuffled]
    return sorted(steps, key=lambda step: -sum(min(d, 4 - d) for d in step[:3]))


def visibility(blocks, r, tm):
    odd = lax.rem(tm, 2)
    lane = lax.broadcasted_iota(jnp.int32, (256, LANES), 1)
    sign = jnp.where(lane < 64, 1.0, -1.0).astype(F32)
    plain = [split(b) for b in blocks]
    turned = [split(pltpu.roll(b, 64, 1) * sign) for b in blocks]
    ph, plo, th, tlo = (jnp.concatenate([b[part] for b in of], axis=1) for of in (plain, turned) for part in (0, 1))
    real = contract(ph, ph) + contract(ph, plo) + contract(plo, ph)
    imag = contract(th, ph) + contract(th, plo) + contract(tlo, ph)
    flip = 1.0 if r == 0 else jnp.where(odd == 1, -1.0, 1.0).astype(F32)
    return jnp.where(odd == 1, (8 - r) % 8, r), real, imag * flip


def tail_kernel(begun, last, out, stage, sem):
    tm = lax.axis_index("tm")
    writes = [pltpu.make_async_copy(begun.at[:, pl.ds(1, 7)], out.at[:, pl.ds(1, 7)], sem.at[0])]
    writes[0].start()
    _, real, imag = visibility([last[0, t] for t in range(4)], 0, tm)
    stage[0] = real
    stage[1] = imag
    writes.append(pltpu.make_async_copy(stage, out.at[:, 0], sem.at[1]))
    writes[-1].start()
    for write in writes:
        write.wait()


def kernel(volt, taps_hbm, table_hbm, out, last, taps, table, ext, tapb, xs, send, recv, load_sem, halo_send, halo_recv, column_sem, send_sem, recv_sem):
    inputs, frames = volt.shape[0], volt.shape[1]
    blocks = volt.shape[2] // LANES
    inp, tm, here = place()
    me = inp * 4 + tm

    high, low = inp // 16 * 16, lax.rem(inp, 16)
    plane = [(high + lax.rem(low + k, 16), tm) for k in range(1, 16)]
    column = [(inp, lax.rem(tm + k, 4)) for k in (1, 2, 3)] + [(lax.rem(inp + 16, 32), lax.rem(tm + k, 4)) for k in range(4)]

    def greet(line, sem):
        for device in line:
            pl.semaphore_signal(sem, inc=1, device_id=device, device_id_type=MESH)

    barrier = pltpu.get_barrier_semaphore()
    greet(column, barrier)
    greet(plane, barrier)

    loads = [
        pltpu.make_async_copy(taps_hbm, taps, load_sem.at[blocks]),
        pltpu.make_async_copy(table_hbm, table, load_sem.at[blocks + 1]),
    ]
    loads[0].start()
    for l in range(blocks):
        lanes = pl.ds(l * LANES, LANES)
        loads.append(pltpu.make_async_copy(volt.at[:, :, lanes], ext.at[:, l, pl.ds(8, frames), :], load_sem.at[l]))
        loads[-1].start()
    loads[1].start()

    pl.semaphore_wait(barrier, 22)
    greet(column, column_sem)
    halos = [
        pltpu.make_async_remote_copy(
            src_ref=volt.at[:, pl.ds(frames - 3, 3), pl.ds(l * LANES, LANES)],
            dst_ref=ext.at[:, l, pl.ds(5, 3), :],
            send_sem=halo_send.at[l],
            recv_sem=halo_recv.at[l],
            device_id=(inp, lax.rem(tm + 1, 4)),
            device_id_type=MESH,
        )
        for l in range(blocks)
    ]

    @pl.when(tm < 3)
    def _():
        for halo in halos:
            halo.start()

    @pl.when(tm == 0)
    def _():
        @pl.loop(0, inputs)
        def _(i):
            for l in range(blocks):
                ext[i, l, 5:8, :] = jnp.zeros((3, LANES), F32)

    loads[0].wait()
    for k in range(4):
        for l in range(blocks):
            tapb[k, l] = jnp.broadcast_to(taps[k : k + 1, l * LANES : (l + 1) * LANES], (8, LANES))
    for load in loads[2:]:
        load.wait()

    step = 16

    def filtered(i, f):
        parts = []
        for l in range(blocks):
            halves = []
            for j in range(step // 8):
                row = 5 + f * step + j * 8
                acc = tapb[0, l] * ext[i, l, pl.ds(row, 8), :]
                for k in range(1, 4):
                    acc = acc + tapb[k, l] * ext[i, l, pl.ds(row + k, 8), :]
                halves.append(acc)
            parts.append(jnp.concatenate(halves, axis=0))
        y = sixteen(parts)
        rows = pl.ds(pl.multiple_of(i * frames, frames) + f * step, step)
        for r in range(9):
            real, imag = y[r]
            high, low = split(real)
            xs[r, 0, 0, rows, :] = high
            xs[r, 1, 0, rows, :] = low
            xs[r, 0, 1, rows, :] = -high
            xs[r, 1, 1, rows, :] = -low
            if imag is not None:
                high, low = split(imag)
                xs[r, 0, 2, rows, :] = high
                xs[r, 1, 2, rows, :] = low

    def later(first, last):
        @pl.loop(first, last)
        def _(i):
            for f in range(1, frames // step):
                filtered(i, f)

    later(0, inputs)

    @pl.when(tm > 0)
    def _():
        for halo in halos:
            halo.wait_recv()

    @pl.loop(0, inputs)
    def _(i):
        filtered(i, 0)

    loads[1].wait()

    def operand(r, part, pair):
        rows_ = []
        for i in (2 * pair, 2 * pair + 1):
            rows = pl.ds(i * frames, frames)
            real, minus = xs[r, part, 0, rows, :], xs[r, part, 1, rows, :]
            imag = jnp.zeros_like(real) if r in (0, 8) else xs[r, part, 2, rows, :]
            rows_.append(jnp.concatenate([real, imag], axis=1))
            rows_.append(jnp.concatenate([imag, minus], axis=1))
        return jnp.concatenate(rows_, axis=0)

    def product(r, pair):
        both = contract(table[r], operand(r, 0, pair))
        return both[:128] + both[128:] + contract(table[r, 0:128], operand(r, 1, pair))

    flat = send.reshape(DEVICES * 64, LANES)

    def fill(r):
        for pair in range(inputs // 2):
            value = product(r, pair)
            if r == 0:
                value = value + product(8, pair)
            for h in range(2):
                flat[pl.ds(r * inputs + 2 * pair + h, DEVICES, stride=64), :] = value[:, h * LANES : (h + 1) * LANES]

    rows = pl.ds(pl.multiple_of(inp * 8, 8), 8)

    def landing(first, count):
        return last.at[pl.ds(0, 1), tm, rows, :] if first == 0 else recv.at[pl.ds(first - 1, count), tm, rows, :]

    def ship(g, to_inp, to_tm):
        first, count = GROUPS[g]
        pltpu.make_async_remote_copy(
            src_ref=send.at[to_inp * 4 + to_tm, pl.ds(first, count)],
            dst_ref=landing(first, count),
            send_sem=send_sem,
            recv_sem=recv_sem.at[g],
            device_id=(to_inp, to_tm),
            device_id_type=MESH,
        ).start()

    x, y, z, core = here
    x_at = [lax.rem(x + j, 4) * 4 for j in range(4)]
    y_at = [lax.rem(y + j, 4) for j in range(4)]
    y_at = [(at // 2 * 16, lax.rem(at, 2) * 2) for at in y_at]
    z_at = [lax.rem(z + j, 4) for j in range(4)]
    core_at = [core, 1 - core]

    def exchange(g):
        first, count = GROUPS[g]
        pltpu.make_async_copy(send.at[me, pl.ds(first, count)], landing(first, count), recv_sem.at[g]).start()
        steps = offsets()
        if g == 0:
            steps = [step for step in steps if step[1] == step[3] == 0] + [step for step in steps if step[1] or step[3]]
        for k, (dx, dy, dz, dc) in enumerate(steps):
            if g == 0 and k == 15:
                pl.semaphore_wait(column_sem, 7)
            ship(g, y_at[dy][0] + x_at[dx] + z_at[dz], y_at[dy][1] + core_at[dc])

    for g, (first, count) in enumerate(GROUPS):
        for r in range(first, first + count):
            fill(r)
        exchange(g)

    for g, (first, count) in enumerate(GROUPS[:-1]):
        slots = recv.at[pl.ds(first - 1, count)]
        pltpu.make_async_copy(slots, slots, recv_sem.at[g]).wait()
        for r in range(first, first + count):
            chan, real, imag = visibility([recv[r - 1, t] for t in range(4)], r, tm)
            out[0, chan] = real
            out[1, chan] = imag
    pltpu.make_async_copy(last, last, recv_sem.at[len(GROUPS) - 1]).wait()
    @pl.when(tm < 3)
    def _():
        for halo in halos:
            halo.wait_send()

    sent = send.at[pl.ds(0, DEVICES - 1)]
    pltpu.make_async_copy(sent, sent, send_sem).wait()


def on_device(voltages, taps):
    inputs, frames, nfft = voltages.shape
    table = jnp.asarray(tables(nfft, 4 * frames))
    vmem = pl.BlockSpec(memory_space=pltpu.VMEM)
    hbm = pl.BlockSpec(memory_space=pltpu.HBM)
    result = jax.ShapeDtypeStruct((2, 8, 256, 256), F32)
    begun, last = pl.pallas_call(
        kernel,
        out_shape=(result, jax.ShapeDtypeStruct((1, 4, 256, LANES), F32)),
        in_specs=[hbm, hbm, hbm],
        out_specs=(vmem, vmem),
        scratch_shapes=[
            pltpu.VMEM(taps.shape, F32),
            pltpu.VMEM(table.shape, BF16),
            pltpu.VMEM((inputs, nfft // LANES, frames + 8, LANES), F32),
            pltpu.VMEM((4, nfft // LANES, 8, LANES), F32),
            pltpu.VMEM((9, 2, 3, inputs * frames, LANES), BF16),
            pltpu.VMEM((DEVICES, 8, inputs, LANES), F32),
            pltpu.VMEM((7, 4, 256, LANES), F32),
            pltpu.SemaphoreType.DMA((nfft // LANES + 2,)),
            pltpu.SemaphoreType.DMA((nfft // LANES,)),
            pltpu.SemaphoreType.DMA((nfft // LANES,)),
            pltpu.SemaphoreType.REGULAR,
            pltpu.SemaphoreType.DMA,
            pltpu.SemaphoreType.DMA((len(GROUPS),)),
        ],
        compiler_params=pltpu.CompilerParams(collective_id=0, has_side_effects=True, vmem_limit_bytes=40 << 20),
    )(*(pltpu.with_memory_space_constraint(v, pltpu.HBM) for v in (voltages, taps, table)))
    return pl.pallas_call(
        tail_kernel,
        out_shape=result,
        in_specs=[vmem, vmem],
        out_specs=hbm,
        scratch_shapes=[pltpu.VMEM((2, 256, 256), F32), pltpu.SemaphoreType.DMA((2,))],
        compiler_params=pltpu.CompilerParams(vmem_limit_bytes=24 << 20),
    )(begun, last)


def solution(mesh):
    return jax.shard_map(
        on_device,
        mesh=mesh,
        in_specs=(P("inp", "tm", None), P()),
        out_specs=P(None, ("inp", "tm"), None, None),
        check_vma=False,
    )
```

```python
import functools
import math

import jax
import jax.numpy as jnp
import numpy as np
from jax import lax
from jax.experimental import pallas as pl
from jax.experimental.pallas import tpu as pltpu
from jax.sharding import PartitionSpec as P

LANES = 128
F32 = jnp.float32
BF16 = jnp.bfloat16


def tables(nfft, spectra):
    dests = 128
    n2 = np.arange(LANES)
    scale = 1.0 / math.sqrt(nfft) / math.sqrt(spectra)
    out = np.zeros((9, dests, 2 * LANES), np.float64)
    for r in range(9):
        for m in range(dests):
            if (r == 0 and m % 2 == 1) or (r == 8 and m % 2 == 0):
                continue
            q = m // 2 if (m % 2 == 0 or r == 8) else 127 - m // 2
            angle = 2.0 * np.pi * ((n2 * (16 * q + r)) % nfft) / nfft
            out[r, m, :LANES] = np.cos(angle) * scale
            out[r, m, LANES:] = np.sin(angle) * scale
    out = out.astype(np.float32)
    high = out.astype(jnp.bfloat16)
    low = (out - high.astype(np.float32)).astype(jnp.bfloat16)
    return np.concatenate([high, low], axis=1)


def split(value):
    high = value.astype(BF16)
    return high, (value - high.astype(F32)).astype(BF16)


def sixteen(x):
    c1, c2, c3 = (math.cos(k * math.pi / 8) for k in (1, 2, 3))
    a = [x[n] + x[n + 8] for n in range(8)]
    b = [x[n] - x[n + 8] for n in range(8)]
    c = [a[n] + a[n + 4] for n in range(4)]
    d = [a[n] - a[n + 4] for n in range(4)]
    c02, c13 = c[0] + c[2], c[1] + c[3]
    y = {0: (c02 + c13, None), 8: (c02 - c13, None), 4: (c[0] - c[2], c[3] - c[1])}
    dm, dp = (d[1] - d[3]) * c2, (d[1] + d[3]) * c2
    y[2] = (d[0] + dm, -(d[2] + dp))
    y[6] = (d[0] - dm, d[2] - dp)
    e = [None] + [b[n] - b[8 - n] for n in (1, 2, 3)]
    g = [None] + [b[n] + b[8 - n] for n in (1, 2, 3)]
    e2, g2 = e[2] * c2, g[2] * c2
    p, q = b[0] + e2, b[0] - e2
    s, t = e[1] * c1 + e[3] * c3, e[1] * c3 - e[3] * c1
    v, w = b[4] + g2, g2 - b[4]
    h, k = g[1] * c3 + g[3] * c1, g[1] * c1 - g[3] * c3
    y[1] = (p + s, -(v + h))
    y[7] = (p - s, v - h)
    y[3] = (q + t, -(k + w))
    y[5] = (q - t, w - k)
    return y


def contract(a, b):
    return lax.dot_general(a, b, (((1,), (1,)), ((), ())), preferred_element_type=F32)


MESH = pl.DeviceIdType.MESH
GROUPS = ((1, 1), (2, 2), (4, 2), (6, 2), (0, 1))
DEVICES = 128


def place():
    inp, tm = lax.axis_index("inp"), lax.axis_index("tm")
    return inp, tm, (lax.rem(inp // 4, 4), inp // 16 * 2 + tm // 2, lax.rem(inp, 4), lax.rem(tm, 2))


def offsets():
    shuffled = np.random.RandomState(1).permutation(np.arange(1, DEVICES))
    steps = [(int(k) // 2 % 4, int(k) // 8 % 4, int(k) // 32, int(k) % 2) for k in shuffled]
    rank = {step: k for k, step in enumerate(steps)}

    def order(step):
        back = tuple((4 - d) % 4 for d in step[:3]) + step[3:]
        return -sum(min(d, 4 - d) for d in step[:3]), min(rank[step], rank[back]), rank[step]

    return sorted(steps, key=order)


def visibility(blocks, r, tm):
    odd = lax.rem(tm, 2)
    lane = lax.broadcasted_iota(jnp.int32, (256, LANES), 1)
    sign = jnp.where(lane < 64, 1.0, -1.0).astype(F32)
    plain = [split(b) for b in blocks]
    turned = [split(pltpu.roll(b, 64, 1) * sign) for b in blocks]
    ph, plo, th, tlo = (jnp.concatenate([b[part] for b in of], axis=1) for of in (plain, turned) for part in (0, 1))
    real = contract(ph, ph) + contract(ph, plo) + contract(plo, ph)
    imag = contract(th, ph) + contract(th, plo) + contract(tlo, ph)
    flip = 1.0 if r == 0 else jnp.where(odd == 1, -1.0, 1.0).astype(F32)
    return jnp.where(odd == 1, (8 - r) % 8, r), real, imag * flip


def tail_kernel(begun, last, out, stage, sem):
    tm = lax.axis_index("tm")
    writes = [pltpu.make_async_copy(begun.at[:, pl.ds(1, 7)], out.at[:, pl.ds(1, 7)], sem.at[0])]
    writes[0].start()
    _, real, imag = visibility([last[0, t] for t in range(4)], 0, tm)
    stage[0] = real
    stage[1] = imag
    writes.append(pltpu.make_async_copy(stage, out.at[:, 0], sem.at[1]))
    writes[-1].start()
    for write in writes:
        write.wait()


def kernel(volt, taps_hbm, table_hbm, out, last, taps, table, ext, tapb, xs, send, recv, load_sem, halo_send, halo_recv, column_sem, send_sem, recv_sem):
    inputs, frames = volt.shape[0], volt.shape[1]
    blocks = volt.shape[2] // LANES
    inp, tm, here = place()
    me = inp * 4 + tm

    high, low = inp // 16 * 16, lax.rem(inp, 16)
    plane = [(high + lax.rem(low + k, 16), tm) for k in range(1, 16)]
    column = [(inp, lax.rem(tm + k, 4)) for k in (1, 2, 3)] + [(lax.rem(inp + 16, 32), lax.rem(tm + k, 4)) for k in range(4)]

    def greet(line, sem):
        for device in line:
            pl.semaphore_signal(sem, inc=1, device_id=device, device_id_type=MESH)

    barrier = pltpu.get_barrier_semaphore()
    greet(column, barrier)
    greet(plane, barrier)

    loads = [
        pltpu.make_async_copy(taps_hbm, taps, load_sem.at[blocks]),
        pltpu.make_async_copy(table_hbm, table, load_sem.at[blocks + 1]),
    ]
    loads[0].start()
    for l in range(blocks):
        lanes = pl.ds(l * LANES, LANES)
        loads.append(pltpu.make_async_copy(volt.at[:, :, lanes], ext.at[:, l, pl.ds(8, frames), :], load_sem.at[l]))
        loads[-1].start()
    loads[1].start()

    pl.semaphore_wait(barrier, 22)
    greet(column, column_sem)
    halos = [
        pltpu.make_async_remote_copy(
            src_ref=volt.at[:, pl.ds(frames - 3, 3), pl.ds(l * LANES, LANES)],
            dst_ref=ext.at[:, l, pl.ds(5, 3), :],
            send_sem=halo_send.at[l],
            recv_sem=halo_recv.at[l],
            device_id=(inp, lax.rem(tm + 1, 4)),
            device_id_type=MESH,
        )
        for l in range(blocks)
    ]

    @pl.when(tm < 3)
    def _():
        for halo in halos:
            halo.start()

    @pl.when(tm == 0)
    def _():
        @pl.loop(0, inputs)
        def _(i):
            for l in range(blocks):
                ext[i, l, 5:8, :] = jnp.zeros((3, LANES), F32)

    loads[0].wait()
    for k in range(4):
        for l in range(blocks):
            tapb[k, l] = jnp.broadcast_to(taps[k : k + 1, l * LANES : (l + 1) * LANES], (8, LANES))
    for load in loads[2:]:
        load.wait()

    step = 16

    def filtered(i, f):
        parts = []
        for l in range(blocks):
            halves = []
            for j in range(step // 8):
                row = 5 + f * step + j * 8
                acc = tapb[0, l] * ext[i, l, pl.ds(row, 8), :]
                for k in range(1, 4):
                    acc = acc + tapb[k, l] * ext[i, l, pl.ds(row + k, 8), :]
                halves.append(acc)
            parts.append(jnp.concatenate(halves, axis=0))
        y = sixteen(parts)
        rows = pl.ds(pl.multiple_of(i * frames, frames) + f * step, step)
        for r in range(9):
            real, imag = y[r]
            high, low = split(real)
            xs[r, 0, 0, rows, :] = high
            xs[r, 1, 0, rows, :] = low
            xs[r, 0, 1, rows, :] = -high
            xs[r, 1, 1, rows, :] = -low
            if imag is not None:
                high, low = split(imag)
                xs[r, 0, 2, rows, :] = high
                xs[r, 1, 2, rows, :] = low

    def later(first, last):
        @pl.loop(first, last)
        def _(i):
            for f in range(1, frames // step):
                filtered(i, f)

    later(0, inputs)

    @pl.when(tm > 0)
    def _():
        for halo in halos:
            halo.wait_recv()

    @pl.loop(0, inputs)
    def _(i):
        filtered(i, 0)

    loads[1].wait()

    def operand(r, part, pair):
        rows_ = []
        for i in (2 * pair, 2 * pair + 1):
            rows = pl.ds(i * frames, frames)
            real, minus = xs[r, part, 0, rows, :], xs[r, part, 1, rows, :]
            imag = jnp.zeros_like(real) if r in (0, 8) else xs[r, part, 2, rows, :]
            rows_.append(jnp.concatenate([real, imag], axis=1))
            rows_.append(jnp.concatenate([imag, minus], axis=1))
        return jnp.concatenate(rows_, axis=0)

    def product(r, pair):
        both = contract(table[r], operand(r, 0, pair))
        return both[:128] + both[128:] + contract(table[r, 0:128], operand(r, 1, pair))

    flat = send.reshape(DEVICES * 64, LANES)

    def fill(r):
        for pair in range(inputs // 2):
            value = product(r, pair)
            if r == 0:
                value = value + product(8, pair)
            for h in range(2):
                flat[pl.ds(r * inputs + 2 * pair + h, DEVICES, stride=64), :] = value[:, h * LANES : (h + 1) * LANES]

    rows = pl.ds(pl.multiple_of(inp * 8, 8), 8)

    def landing(first, count):
        return last.at[pl.ds(0, 1), tm, rows, :] if first == 0 else recv.at[pl.ds(first - 1, count), tm, rows, :]

    def ship(g, to_inp, to_tm):
        first, count = GROUPS[g]
        pltpu.make_async_remote_copy(
            src_ref=send.at[to_inp * 4 + to_tm, pl.ds(first, count)],
            dst_ref=landing(first, count),
            send_sem=send_sem,
            recv_sem=recv_sem.at[g],
            device_id=(to_inp, to_tm),
            device_id_type=MESH,
        ).start()

    x, y, z, core = here
    x_at = [lax.rem(x + j, 4) * 4 for j in range(4)]
    y_at = [lax.rem(y + j, 4) for j in range(4)]
    y_at = [(at // 2 * 16, lax.rem(at, 2) * 2) for at in y_at]
    z_at = [lax.rem(z + j, 4) for j in range(4)]
    core_at = [core, 1 - core]

    def exchange(g):
        first, count = GROUPS[g]
        pltpu.make_async_copy(send.at[me, pl.ds(first, count)], landing(first, count), recv_sem.at[g]).start()
        steps = offsets()
        if g == 0:
            steps = [step for step in steps if step[1] == step[3] == 0] + [step for step in steps if step[1] or step[3]]
        for k, (dx, dy, dz, dc) in enumerate(steps):
            if g == 0 and k == 15:
                pl.semaphore_wait(column_sem, 7)
            ship(g, y_at[dy][0] + x_at[dx] + z_at[dz], y_at[dy][1] + core_at[dc])

    for g, (first, count) in enumerate(GROUPS):
        for r in range(first, first + count):
            fill(r)
        exchange(g)

    for g, (first, count) in enumerate(GROUPS[:-1]):
        slots = recv.at[pl.ds(first - 1, count)]
        pltpu.make_async_copy(slots, slots, recv_sem.at[g]).wait()
        for r in range(first, first + count):
            chan, real, imag = visibility([recv[r - 1, t] for t in range(4)], r, tm)
            out[0, chan] = real
            out[1, chan] = imag
    pltpu.make_async_copy(last, last, recv_sem.at[len(GROUPS) - 1]).wait()
    @pl.when(tm < 3)
    def _():
        for halo in halos:
            halo.wait_send()

    sent = send.at[pl.ds(0, DEVICES - 1)]
    pltpu.make_async_copy(sent, sent, send_sem).wait()


def on_device(voltages, taps):
    inputs, frames, nfft = voltages.shape
    table = jnp.asarray(tables(nfft, 4 * frames))
    vmem = pl.BlockSpec(memory_space=pltpu.VMEM)
    hbm = pl.BlockSpec(memory_space=pltpu.HBM)
    result = jax.ShapeDtypeStruct((2, 8, 256, 256), F32)
    begun, last = pl.pallas_call(
        kernel,
        out_shape=(result, jax.ShapeDtypeStruct((1, 4, 256, LANES), F32)),
        in_specs=[hbm, hbm, hbm],
        out_specs=(vmem, vmem),
        scratch_shapes=[
            pltpu.VMEM(taps.shape, F32),
            pltpu.VMEM(table.shape, BF16),
            pltpu.VMEM((inputs, nfft // LANES, frames + 8, LANES), F32),
            pltpu.VMEM((4, nfft // LANES, 8, LANES), F32),
            pltpu.VMEM((9, 2, 3, inputs * frames, LANES), BF16),
            pltpu.VMEM((DEVICES, 8, inputs, LANES), F32),
            pltpu.VMEM((7, 4, 256, LANES), F32),
            pltpu.SemaphoreType.DMA((nfft // LANES + 2,)),
            pltpu.SemaphoreType.DMA((nfft // LANES,)),
            pltpu.SemaphoreType.DMA((nfft // LANES,)),
            pltpu.SemaphoreType.REGULAR,
            pltpu.SemaphoreType.DMA,
            pltpu.SemaphoreType.DMA((len(GROUPS),)),
        ],
        compiler_params=pltpu.CompilerParams(collective_id=0, has_side_effects=True, vmem_limit_bytes=40 << 20),
    )(*(pltpu.with_memory_space_constraint(v, pltpu.HBM) for v in (voltages, taps, table)))
    return pl.pallas_call(
        tail_kernel,
        out_shape=result,
        in_specs=[vmem, vmem],
        out_specs=hbm,
        scratch_shapes=[pltpu.VMEM((2, 256, 256), F32), pltpu.SemaphoreType.DMA((2,))],
        compiler_params=pltpu.CompilerParams(vmem_limit_bytes=24 << 20),
    )(begun, last)


def solution(mesh):
    return jax.shard_map(
        on_device,
        mesh=mesh,
        in_specs=(P("inp", "tm", None), P()),
        out_specs=P(None, ("inp", "tm"), None, None),
        check_vma=False,
    )
```
